128 devices in a mesh: section: 4 (over x), seq: 32 (over z, y, core).
Axes of the slice: x: 4, y: 4, z: 4, core: 2. Of those that a mesh axis runs over, the one named last changes fastest.
Arguments:
- latents: bfloat16 [2, 1280, 1536], P(None, 'seq'), may hold values from -6 to 6
- lengths: int32 [2], replicated, may hold values from 1 to 1280, as said below
- segment_layers: int32 [4], P('section'), may hold values from 1 to 2, as said below
- norm_gain: bfloat16 [8, 1536], P('section'), may hold values from 0.3984375 to 1.59375
- qkv_weight: bfloat16 [8, 1536, 2304], P('section'), may hold values from -0.15625 to 0.15625
- qk_gain: bfloat16 [8, 128], P('section'), may hold values from 0.25 to 1.75
- out_weight: bfloat16 [8, 768, 1536], P('section'), may hold values from -0.21875 to 0.21875
Outputs:
- denoised: bfloat16 [2, 1280, 1536], P(None, 'seq', 'section')
The draws below stay inside these ranges and needn't reach their ends.
Inputs may be any that keep to these rules, and one draw needn't show every extreme that they name: `lengths`: one micro-batch in every draw has all 1280 tokens live. `segment_layers`: some section runs all 2 slots and some section runs one.
All inputs are finite; a program needn't handle non-finite values.
Results may differ from the reference program's by a relative error of at most 0.023.
Values may be sent and summed in bfloat16 or wider, within the bound.
A program may use at most 128 MiB of HBM per device.

```python
import jax
import jax.numpy as jnp
from jax import lax

D = 1536
HDIM = 64
SLOTS = 2
MICRO = 2
HD = 768
SEQ = 1280
LAYERS = 8
N_SECTION = 4


def draw_lengths(key, part):
    key_len = jax.random.fold_in(key, 11)
    key_pick = jax.random.fold_in(key, 12)
    drawn = jax.random.randint(key_len, (MICRO,), 1, SEQ + 1)
    picked = jax.random.randint(key_pick, (), 0, MICRO)
    return jnp.where(jnp.arange(MICRO) == picked, SEQ, drawn).astype(jnp.int32)


def draw_segment_layers(key, part):
    key_count = jax.random.fold_in(key, 21)
    key_pick = jax.random.fold_in(key, 22)
    drawn = jax.random.randint(key_count, (N_SECTION,), 1, SLOTS + 1)
    picked = jax.random.randint(key_pick, (), 0, N_SECTION)
    positions = jnp.arange(N_SECTION)
    drawn = jnp.where(positions == picked, SLOTS, drawn)
    drawn = jnp.where(positions == (picked + 1) % N_SECTION, 1, drawn)
    return drawn.astype(jnp.int32)


def block_scale(own_key, shape, shards, low, top_value):
    level = 1.0
    for dim, blocks in shards:
        draws = jax.random.uniform(jax.random.fold_in(jax.random.fold_in(own_key, 6), dim), (blocks,), jnp.float32, low / len(shards), top_value / len(shards))
        level = level * jnp.repeat(jnp.exp(draws), shape[dim] // blocks).reshape((-1,) + (1,) * (len(shape) - 1 - dim))
    return level


def normal_values(stream_key, extent, deviation, bound, pieces=(), kind=jnp.bfloat16):
    array = deviation * jax.random.normal(stream_key, extent, jnp.float32)
    if pieces:
        array = array * block_scale(stream_key, extent, pieces, -0.22, 0.18)
    return jnp.clip(array, -bound, bound).astype(kind)


def setup_inputs(seed: int = 0) -> dict:
    arg_keys = jax.random.split(jax.random.key(seed), 8)
    latents = normal_values(arg_keys[0], (MICRO, SEQ, D), 1.0, 6.0, ((1, 32),))
    lengths = draw_lengths(jax.random.fold_in(arg_keys[7], 71), 0)
    segment_layers = draw_segment_layers(jax.random.fold_in(arg_keys[7], 71), 0)
    norm_gain = jnp.clip(1.0 + 0.12 * jax.random.normal(arg_keys[3], (LAYERS, D), jnp.float32), 0.3984375, 1.59375).astype(jnp.bfloat16)
    qkv_weight = normal_values(arg_keys[4], (LAYERS, D, 3 * HD), D ** -0.5, 0.15625, ((0, 4),))
    qk_gain = jnp.clip(1.0 + 0.15 * jax.random.normal(arg_keys[5], (LAYERS, 2 * HDIM), jnp.float32), 0.25, 1.75).astype(jnp.bfloat16)
    out_weight = normal_values(arg_keys[6], (LAYERS, HD, D), HD ** -0.5, 0.21875, ((0, 4),))
    return dict(latents=latents, lengths=lengths, segment_layers=segment_layers, norm_gain=norm_gain, qkv_weight=qkv_weight, qk_gain=qk_gain, out_weight=out_weight)


eps_norm = 1e-06
neg_large = -1e+30

def rms_scale(values, gain_vec):
    return values * lax.rsqrt(lax.optimization_barrier(jnp.mean(values * values, axis=-1, keepdims=True)) + eps_norm) * gain_vec

def rounded(values):
    return lax.optimization_barrier(values.astype(jnp.bfloat16)).astype(jnp.float32)

def attention_layer(current, length, norm_w, qkv_w, qk_w, out_w):
    seq_rows, width = current.shape
    inner = qkv_w.shape[1] // 3
    head_dim = qk_w.shape[0] // 2
    head_count = inner // head_dim
    resid = current.astype(jnp.float32)
    normed = rms_scale(resid, norm_w.astype(jnp.float32)).astype(jnp.bfloat16)
    projected = jnp.dot(normed, qkv_w, preferred_element_type=jnp.float32)
    queries = rounded(rms_scale(projected[:, :inner].reshape(seq_rows, head_count, head_dim), qk_w[:head_dim].astype(jnp.float32)))
    keys = rounded(rms_scale(projected[:, inner:2 * inner].reshape(seq_rows, head_count, head_dim), qk_w[head_dim:].astype(jnp.float32)))
    values = rounded(projected[:, 2 * inner:].reshape(seq_rows, head_count, head_dim))
    scores = jnp.einsum('qhd,khd->hqk', queries, keys) * head_dim ** (-0.5)
    key_mask = jnp.arange(seq_rows, dtype=jnp.int32) < length
    scores = jnp.where(key_mask[None, None, :], scores, neg_large)
    top_score = lax.optimization_barrier(jnp.max(scores, axis=-1, keepdims=True))
    weights = jnp.exp(scores - top_score)
    totals = lax.optimization_barrier(jnp.sum(weights, axis=-1))
    mixed = jnp.einsum('hqk,khd->hqd', rounded(weights), values)
    attended = rounded(mixed / totals[..., None])
    update = jnp.einsum('hqd,hde->qe', attended, out_w.reshape(head_count, head_dim, width).astype(jnp.float32))
    return (resid + update).astype(jnp.bfloat16)

def reference(latents, lengths, segment_layers, norm_gain, qkv_weight, qk_gain, out_weight):
    layer_ids = jnp.arange(qkv_weight.shape[0], dtype=jnp.int32)
    active = layer_ids % SLOTS < segment_layers[layer_ids // SLOTS]

    def run_micro(inputs):
        sample, length = inputs

        def step_layer(current, layer_in):
            flag, norm_w, qkv_w, qk_w, out_w = layer_in
            updated = attention_layer(current, length, norm_w, qkv_w, qk_w, out_w)
            return (jnp.where(flag, updated, current), None)
        final_x, unused = lax.scan(step_layer, sample, (active, norm_gain, qkv_weight, qk_gain, out_weight))
        return final_x
    return lax.map(run_micro, (latents, lengths))
```

```python
import functools
import itertools
import math

import jax
import jax.numpy as jnp
from jax import lax
from jax.experimental import pallas as pl
from jax.experimental.pallas import tpu as pltpu
from jax.sharding import PartitionSpec as P

MESH = pl.DeviceIdType.MESH
EPS = 1e-06
MICRO, ROWS, D = 2, 40, 1536
HEADS, HDIM, INNER = 12, 64, 768
CHIPS, SECTIONS, SLOTS = 16, 4, 2
TOK = 2 * ROWS
SEQ = CHIPS * TOK
ROWS_A, ROWS_B = 48, 32
GROUP = 256
OUT_COLS = D // SECTIONS
LOG2E = math.log2(math.e)
TOP = 25.0
SCALE = HDIM**-0.5
BLOCKS = 4
CHUNKS = CHIPS // BLOCKS


def place():
    seq = lax.axis_index("seq")
    return lax.axis_index("section"), seq // 2, seq % 2


def device(section, chip, core):
    return (section, chip * 2 + core)


def start_gather(latents_ref, count_ref, x_ref, counts_ref, own, count_send, x_ss, x_rs, c_ss, c_rs):
    section, chip, core = place()
    barrier = pltpu.get_barrier_semaphore()
    pl.semaphore_signal(barrier, inc=1, device_id=device(section, chip, 1 - core), device_id_type=MESH)
    for step in range(1, SECTIONS):
        pl.semaphore_signal(
            barrier, inc=1, device_id=device((section + step) % SECTIONS, chip, core), device_id_type=MESH
        )
    count_send[...] = jnp.full(count_send.shape, count_ref[0], jnp.int32)
    pl.semaphore_wait(barrier, SECTIONS)
    sends = []
    for step in range(1, SECTIONS):
        sends.append(
            pltpu.make_async_remote_copy(
                src_ref=count_send,
                dst_ref=counts_ref.at[section],
                send_sem=c_ss.at[step - 1],
                recv_sem=c_rs,
                device_id=device((section + step) % SECTIONS, chip, core),
                device_id_type=MESH,
            )
        )
    swap = pltpu.make_async_remote_copy(
        src_ref=latents_ref.at[1 - core],
        dst_ref=x_ref.at[core],
        send_sem=x_ss,
        recv_sem=x_rs,
        device_id=device(section, chip, 1 - core),
        device_id_type=MESH,
    )
    for copy in sends:
        copy.start()
    swap.start()
    mine = pltpu.make_async_copy(latents_ref.at[core], x_ref.at[core], own)
    mine.start()
    local = pltpu.make_async_copy(count_send, counts_ref.at[section], c_rs)
    local.start()
    mine.wait()
    for copy in sends:
        copy.wait_send()
    pltpu.make_async_copy(counts_ref, counts_ref, c_rs).wait()
    swap.wait()


def gather_call(latents, counts):
    return pl.pallas_call(
        start_gather,
        name="gather_start",
        out_shape=(
            jax.ShapeDtypeStruct((2, ROWS, D), jnp.bfloat16),
            jax.ShapeDtypeStruct((SECTIONS, 8, 128), jnp.int32),
        ),
        in_specs=[pl.BlockSpec(memory_space=pltpu.VMEM), pl.BlockSpec(memory_space=pltpu.SMEM)],
        out_specs=(pl.BlockSpec(memory_space=pltpu.VMEM),) * 2,
        scratch_shapes=[
            pltpu.SemaphoreType.DMA,
            pltpu.VMEM((8, 128), jnp.int32),
            pltpu.SemaphoreType.DMA,
            pltpu.SemaphoreType.DMA,
            pltpu.SemaphoreType.DMA((SECTIONS - 1,)),
            pltpu.SemaphoreType.DMA,
        ],
        compiler_params=pltpu.CompilerParams(collective_id=0, has_side_effects=True),
    )(latents, counts)


def relay(
    counts,
    len_ref,
    x0_ref,
    ng_ref,
    wqkv_hbm,
    qkg_ref,
    wo_hbm,
    o_ref,
    wqkv,
    wo,
    x,
    xn,
    snd,
    rcv,
    kve,
    bias,
    bdiag,
    rsnd,
    ret,
    att,
    osnd,
    orcv,
    w_sem,
    s_ss,
    s_rs,
    r_ss,
    r_rs,
    h_ss,
    h_rs,
    o_ss,
    o_rs,
):
    section, chip, core = place()
    head = (chip + 8 * core) % CHIPS

    barrier = pltpu.get_barrier_semaphore()

    @pl.loop(1, CHIPS)
    def _(step):
        pl.semaphore_signal(
            barrier, inc=1, device_id=device(section, (chip + step) % CHIPS, core), device_id_type=MESH
        )

    for step in range(1, SECTIONS):
        for other in range(2):
            pl.semaphore_signal(
                barrier, inc=1, device_id=device((section + step) % SECTIONS, chip, other), device_id_type=MESH
            )
    pl.semaphore_signal(barrier, inc=1, device_id=device(section, chip, 1 - core), device_id_type=MESH)

    active = 0
    for index, count in enumerate(counts):
        active = jnp.where(section == index, count, active)

    def weight_copies(slot, group):
        span = pl.ds(pl.multiple_of(group * GROUP, GROUP), GROUP)
        return [
            pltpu.make_async_copy(
                wqkv_hbm.at[slot, :, pl.ds(pl.multiple_of(part * INNER + group * GROUP, GROUP), GROUP)],
                wqkv.at[slot, :, pl.ds(pl.multiple_of(part * INNER + group * GROUP, GROUP), GROUP)],
                w_sem.at[slot, group, part],
            )
            for part in range(3)
        ]

    def out_copy(slot):
        return pltpu.make_async_copy(wo_hbm.at[slot], wo.at[slot], w_sem.at[slot, 3, 0])

    @pl.loop(0, active)
    def _(slot):
        @pl.loop(0, 3)
        def _(group):
            for copy in weight_copies(slot, group):
                copy.start()

        out_copy(slot).start()

    length = len_ref[core]
    token = lax.broadcasted_iota(jnp.int32, (8, SEQ), 1)
    bias[...] = jnp.where(token < length, -TOP * LOG2E, -1e30)
    blk_r = lax.broadcasted_iota(jnp.int32, (GROUP, GROUP), 0) // HDIM
    blk_c = lax.broadcasted_iota(jnp.int32, (GROUP, GROUP), 1) // HDIM
    bdiag[...] = jnp.where(blk_r == blk_c, 1.0 / HDIM, 0.0).astype(jnp.bfloat16)
    kve[:, 128:] = jnp.ones((SEQ, 128), jnp.bfloat16)

    def low(rows):
        return lax.broadcasted_iota(jnp.int32, (rows, 128), 1) < HDIM

    def swapped(value):
        return pltpu.roll(value, HDIM, 1)

    pl.semaphore_wait(barrier, CHIPS - 1 + 2 * (SECTIONS - 1) + 1)

    @pl.when(section == 0)
    def _():
        x[0:ROWS, :] = x0_ref[0].astype(jnp.float32)
        x[ROWS:TOK, :] = x0_ref[1].astype(jnp.float32)

    @pl.when(section > 0)
    def _():
        pltpu.make_async_copy(xn, xn, h_rs).wait()
        x[...] = xn[...].astype(jnp.float32)

    def send_copy(par, h):
        target = (h + 8 * core) % CHIPS
        return target, pltpu.make_async_remote_copy(
            src_ref=snd.at[h],
            dst_ref=rcv.at[par, chip],
            send_sem=s_ss.at[h],
            recv_sem=s_rs.at[par],
            device_id=device(section, target, core),
            device_id_type=MESH,
        )

    def return_copy(block):
        return pltpu.make_async_remote_copy(
            src_ref=rsnd.at[block],
            dst_ref=ret.at[head],
            send_sem=r_ss.at[block],
            recv_sem=r_rs,
            device_id=device(section, block, core),
            device_id_type=MESH,
        )

    @pl.loop(0, active)
    def _(slot):
        par = slot
        xv = x[...]
        mean = jnp.mean(xv * xv, axis=-1, keepdims=True)
        gains = ng_ref[...].astype(jnp.float32)
        gain = jnp.where(slot == 0, gains[0:1], gains[1:2])
        xn[...] = (xv * lax.rsqrt(mean + EPS) * gain).astype(jnp.bfloat16)
        qks = qkg_ref[...].astype(jnp.float32)
        qk = jnp.where(slot == 0, qks[0:1], qks[1:2])
        gq = jnp.concatenate([qk[:, :HDIM]] * 4, axis=1)
        gk = jnp.concatenate([qk[:, HDIM:]] * 4, axis=1)

        @pl.loop(0, 3)
        def _(group):
            for copy in weight_copies(slot, group):
                copy.wait()
            xb = xn[...]
            parts = []
            for part in range(3):
                span = pl.ds(pl.multiple_of(part * INNER + group * GROUP, GROUP), GROUP)
                parts.append(jnp.dot(xb, wqkv[slot, :, span], preferred_element_type=jnp.float32))
            q, k, v = parts
            squares = jnp.concatenate([q * q, k * k], axis=0)
            high = squares.astype(jnp.bfloat16)
            rest = (squares - high.astype(jnp.float32)).astype(jnp.bfloat16)
            blocks = bdiag[...]
            means = jnp.dot(high, blocks, preferred_element_type=jnp.float32) + jnp.dot(
                rest, blocks, preferred_element_type=jnp.float32
            )
            inv = lax.rsqrt(means + EPS)
            q = q * inv[:TOK] * gq
            k = k * inv[TOK:] * gk
            for pair in range(2):
                cols = slice(128 * pair, 128 * pair + 128)
                qp, kp, vp = q[:, cols], k[:, cols], v[:, cols]
                kr, vr, qr = swapped(kp), swapped(vp), swapped(qp)
                lo = low(TOK)
                even = jnp.where(lo, kp, vr)
                odd = jnp.where(lo, kr, vp)
                lob = low(ROWS_B)
                q_even = jnp.concatenate(
                    [jnp.where(lob, qp[:ROWS_B], qr[ROWS_A:]), qp[ROWS_B:ROWS_A]], axis=0
                )
                q_odd = jnp.concatenate(
                    [jnp.where(lob, qr[:ROWS_B], qp[ROWS_A:]), qr[ROWS_B:ROWS_A]], axis=0
                )
                for parity, (kv, qq) in enumerate(((even, q_even), (odd, q_odd))):
                    h = 4 * group + 2 * pair + parity
                    snd[h, 0:TOK, :] = kv.astype(jnp.bfloat16)
                    snd[h, TOK:128, :] = qq.astype(jnp.bfloat16)
            for local in range(4):
                h = 4 * group + local
                target, copy = send_copy(par, h)

                @pl.when(target != chip)
                def _():
                    copy.start()

                @pl.when(target == chip)
                def _():
                    pltpu.make_async_copy(snd.at[h], rcv.at[par, chip], s_rs.at[par]).start()

        @pl.when(head < HEADS)
        def _():
            pltpu.make_async_copy(rcv.at[par], rcv.at[par], s_rs.at[par]).wait()
            kve[:, 0:128] = rcv[par, :, 0:TOK, :].reshape(SEQ, 128)

            @pl.loop(0, CHUNKS)
            def _(chunk):
                first = chunk * BLOCKS
                qp = rcv[par, pl.ds(first, BLOCKS), TOK:128, :].astype(jnp.float32)
                qa = qp.reshape(BLOCKS * ROWS_A, 128)
                qb = swapped(qp[:, :ROWS_B, :].reshape(BLOCKS * ROWS_B, 128))
                qs = jnp.concatenate([qa, qb], axis=0)
                qs = jnp.where(low(BLOCKS * TOK), qs, 0.0).astype(jnp.bfloat16)
                scores = lax.dot_general(
                    qs, kve[:, 0:128], (((1,), (1,)), ((), ())), preferred_element_type=jnp.float32
                )
                weights = jnp.exp2(scores * (SCALE * LOG2E) + bias[0:1, :]).astype(jnp.bfloat16)
                mixed = jnp.dot(weights, kve[...], preferred_element_type=jnp.float32)
                out = mixed[:, :128] / mixed[:, 128:]
                for local in range(BLOCKS):
                    block = first + local
                    oa = swapped(out[ROWS_A * local : ROWS_A * (local + 1)])
                    base = BLOCKS * ROWS_A + ROWS_B * local
                    ob = out[base : base + ROWS_B]
                    rsnd[block, 0:ROWS_B, :] = jnp.where(low(ROWS_B), oa[:ROWS_B], ob).astype(jnp.bfloat16)
                    rsnd[block, ROWS_B:ROWS_A, :] = oa[ROWS_B:].astype(jnp.bfloat16)
                for local in range(BLOCKS):
                    block = first + local

                    @pl.when(block != chip)
                    def _():
                        return_copy(block).start()

                    @pl.when(block == chip)
                    def _():
                        pltpu.make_async_copy(rsnd.at[block], ret.at[head], r_rs).start()

        out_copy(slot).wait()
        pltpu.make_async_copy(ret, ret, r_rs).wait()
        for pair in range(HEADS // 2):
            r0 = ret[2 * pair].astype(jnp.float32)
            r1 = ret[2 * pair + 1].astype(jnp.float32)
            cols = slice(128 * pair, 128 * pair + 128)
            att[0:ROWS_A, cols] = jnp.where(low(ROWS_A), r0, swapped(r1)).astype(jnp.bfloat16)
            att[ROWS_A:TOK, cols] = jnp.where(
                low(ROWS_B), swapped(r0)[:ROWS_B], r1[:ROWS_B]
            ).astype(jnp.bfloat16)

        @pl.loop(0, 3)
        def _(group):
            span = pl.ds(pl.multiple_of(group * 512, 512), 512)
            update = jnp.dot(att[...], wo[slot, :, span], preferred_element_type=jnp.float32)
            x[:, span] = (x[:, span] + update).astype(jnp.bfloat16).astype(jnp.float32)

        @pl.loop(0, HEADS)
        def _(h):
            target, copy = send_copy(par, h)

            @pl.when(target != chip)
            def _():
                copy.wait_send()

        @pl.when(head < HEADS)
        def _():
            @pl.loop(0, CHIPS)
            def _(block):
                @pl.when(block != chip)
                def _():
                    return_copy(block).wait_send()

    @pl.when(section < SECTIONS - 1)
    def _():
        xn[...] = x[...].astype(jnp.bfloat16)
        hop = pltpu.make_async_remote_copy(
            src_ref=xn,
            dst_ref=xn,
            send_sem=h_ss,
            recv_sem=h_rs,
            device_id=device((section + 1) % SECTIONS, chip, core),
            device_id_type=MESH,
        )
        hop.start()
        hop.wait_send()

    @pl.when(section == SECTIONS - 1)
    def _():
        copies = []
        for owner in range(2):
            for part in range(SECTIONS):
                osnd[owner, part] = x[
                    owner * ROWS : (owner + 1) * ROWS, part * OUT_COLS : (part + 1) * OUT_COLS
                ].astype(jnp.bfloat16)
        for part in range(SECTIONS - 1):
            for owner in range(2):
                copies.append(
                    pltpu.make_async_remote_copy(
                        src_ref=osnd.at[owner, part],
                        dst_ref=orcv.at[core],
                        send_sem=o_ss.at[owner, part],
                        recv_sem=o_rs,
                        device_id=device(part, chip, owner),
                        device_id_type=MESH,
                    )
                )
        last = SECTIONS - 1
        copies.append(
            pltpu.make_async_remote_copy(
                src_ref=osnd.at[1 - core, last],
                dst_ref=orcv.at[core],
                send_sem=o_ss.at[0, last],
                recv_sem=o_rs,
                device_id=device(last, chip, 1 - core),
                device_id_type=MESH,
            )
        )
        for copy in copies:
            copy.start()
        pltpu.make_async_copy(osnd.at[core, last], orcv.at[core], o_rs).start()
        for copy in copies:
            copy.wait_send()

    pltpu.make_async_copy(orcv, orcv, o_rs).wait()
    o_ref[...] = orcv[...]


def relay_call(counts, cid, lengths, x0, norm_gain, qkv_weight, qk_gain, out_weight):
    vmem = pl.BlockSpec(memory_space=pltpu.VMEM)
    hbm = pl.BlockSpec(memory_space=pl.ANY)
    dma = pltpu.SemaphoreType.DMA
    bf16, f32 = jnp.bfloat16, jnp.float32
    return pl.pallas_call(
        functools.partial(relay, counts),
        name="relay_" + "".join(str(n) for n in counts),
        out_shape=jax.ShapeDtypeStruct((MICRO, ROWS, OUT_COLS), bf16),
        in_specs=[pl.BlockSpec(memory_space=pltpu.SMEM), vmem, vmem, hbm, vmem, hbm],
        out_specs=vmem,
        scratch_shapes=[
            pltpu.VMEM((SLOTS, D, 3 * INNER), bf16),
            pltpu.VMEM((SLOTS, INNER, D), bf16),
            pltpu.VMEM((TOK, D), f32),
            pltpu.VMEM((TOK, D), bf16),
            pltpu.VMEM((HEADS, 128, 128), bf16),
            pltpu.VMEM((2, CHIPS, 128, 128), bf16),
            pltpu.VMEM((SEQ, 256), bf16),
            pltpu.VMEM((8, SEQ), f32),
            pltpu.VMEM((GROUP, GROUP), bf16),
            pltpu.VMEM((CHIPS, ROWS_A, 128), bf16),
            pltpu.VMEM((HEADS, ROWS_A, 128), bf16),
            pltpu.VMEM((TOK, INNER), bf16),
            pltpu.VMEM((2, SECTIONS, ROWS, OUT_COLS), bf16),
            pltpu.VMEM((2, ROWS, OUT_COLS), bf16),
            dma((SLOTS, 4, 3)),
            dma((HEADS,)),
            dma((2,)),
            dma((CHIPS,)),
            dma,
            dma,
            dma,
            dma((2, SECTIONS)),
            dma,
        ],
        compiler_params=pltpu.CompilerParams(
            collective_id=cid, has_side_effects=True, vmem_limit_bytes=56 * 1024 * 1024
        ),
    )(lengths, x0, norm_gain, qkv_weight, qk_gain, out_weight)


PATTERNS = [p for p in itertools.product((1, 2), repeat=SECTIONS) if 1 in p and 2 in p]


def local(latents, lengths, segment_layers, norm_gain, qkv_weight, qk_gain, out_weight):
    x0, gathered = gather_call(latents, segment_layers)
    twos = gathered[:, 0, 0] > 1
    code = jnp.sum(jnp.where(twos, jnp.array([8, 4, 2, 1], jnp.int32), 0))
    index = jnp.clip(code - 1, 0, len(PATTERNS) - 1)
    branches = [functools.partial(relay_call, p, i + 1) for i, p in enumerate(PATTERNS)]
    return lax.switch(index, branches, lengths, x0, norm_gain, qkv_weight, qk_gain, out_weight)


def solution(mesh):
    return jax.shard_map(
        local,
        mesh=mesh,
        in_specs=(
            P(None, "seq", None),
            P(),
            P("section"),
            P("section", None),
            P("section", None, None),
            P("section", None),
            P("section", None, None),
        ),
        out_specs=P(None, "seq", "section"),
        check_vma=False,
    )
```

```python
import functools
import itertools
import math

import jax
import jax.numpy as jnp
from jax import lax
from jax.experimental import pallas as pl
from jax.experimental.pallas import tpu as pltpu
from jax.sharding import PartitionSpec as P

MESH = pl.DeviceIdType.MESH
EPS = 1e-06
MICRO, ROWS, D = 2, 40, 1536
HEADS, HDIM, INNER = 12, 64, 768
CHIPS, SECTIONS, SLOTS = 16, 4, 2
TOK = 2 * ROWS
SEQ = CHIPS * TOK
ROWS_A, ROWS_B = 48, 32
GROUP = 256
OUT_COLS = D // SECTIONS
LOG2E = math.log2(math.e)
SCALE = HDIM**-0.5
BLOCKS = 4
CHUNKS = CHIPS // BLOCKS


def place():
    seq = lax.axis_index("seq")
    return lax.axis_index("section"), seq // 2, seq % 2


def device(section, chip, core):
    return (section, chip * 2 + core)


def start_gather(latents_ref, count_ref, x_ref, counts_ref, own, count_send, x_ss, x_rs, c_ss, c_rs):
    section, chip, core = place()
    barrier = pltpu.get_barrier_semaphore()
    pl.semaphore_signal(barrier, inc=1, device_id=device(section, chip, 1 - core), device_id_type=MESH)
    for step in range(1, SECTIONS):
        pl.semaphore_signal(
            barrier, inc=1, device_id=device((section + step) % SECTIONS, chip, core), device_id_type=MESH
        )
    count_send[...] = jnp.full(count_send.shape, count_ref[0], jnp.int32)
    pl.semaphore_wait(barrier, SECTIONS)
    sends = []
    for step in range(1, SECTIONS):
        sends.append(
            pltpu.make_async_remote_copy(
                src_ref=count_send,
                dst_ref=counts_ref.at[section],
                send_sem=c_ss.at[step - 1],
                recv_sem=c_rs,
                device_id=device((section + step) % SECTIONS, chip, core),
                device_id_type=MESH,
            )
        )
    swap = pltpu.make_async_remote_copy(
        src_ref=latents_ref.at[1 - core],
        dst_ref=x_ref.at[core],
        send_sem=x_ss,
        recv_sem=x_rs,
        device_id=device(section, chip, 1 - core),
        device_id_type=MESH,
    )
    for copy in sends:
        copy.start()
    swap.start()
    mine = pltpu.make_async_copy(latents_ref.at[core], x_ref.at[core], own)
    mine.start()
    local = pltpu.make_async_copy(count_send, counts_ref.at[section], c_rs)
    local.start()
    mine.wait()
    for copy in sends:
        copy.wait_send()
    pltpu.make_async_copy(counts_ref, counts_ref, c_rs).wait()
    swap.wait()


def gather_call(latents, counts):
    return pl.pallas_call(
        start_gather,
        name="gather_start",
        out_shape=(
            jax.ShapeDtypeStruct((2, ROWS, D), jnp.bfloat16),
            jax.ShapeDtypeStruct((SECTIONS, 8, 128), jnp.int32),
        ),
        in_specs=[pl.BlockSpec(memory_space=pltpu.VMEM), pl.BlockSpec(memory_space=pltpu.SMEM)],
        out_specs=(pl.BlockSpec(memory_space=pltpu.VMEM),) * 2,
        scratch_shapes=[
            pltpu.SemaphoreType.DMA,
            pltpu.VMEM((8, 128), jnp.int32),
            pltpu.SemaphoreType.DMA,
            pltpu.SemaphoreType.DMA,
            pltpu.SemaphoreType.DMA((SECTIONS - 1,)),
            pltpu.SemaphoreType.DMA,
        ],
        compiler_params=pltpu.CompilerParams(collective_id=0, has_side_effects=True),
    )(latents, counts)


def relay(
    counts,
    len_ref,
    x0_ref,
    ng_ref,
    wqkv_hbm,
    qkg_ref,
    wo_hbm,
    o_ref,
    wqkv,
    wo,
    x,
    xn,
    snd,
    rcv,
    kve,
    bdiag,
    rsnd,
    ret,
    att,
    osnd,
    orcv,
    w_sem,
    s_ss,
    s_rs,
    r_ss,
    r_rs,
    h_ss,
    h_rs,
    o_ss,
    o_rs,
):
    section, chip, core = place()
    head = (chip + 8 * core) % CHIPS
    row = chip // BLOCKS
    first_group = ((row + 2 * core) % 4 + 1) % 3

    barrier = pltpu.get_barrier_semaphore()

    @pl.loop(1, CHIPS)
    def _(step):
        pl.semaphore_signal(
            barrier, inc=1, device_id=device(section, (chip + step) % CHIPS, core), device_id_type=MESH
        )

    for step in range(1, SECTIONS):
        for other in range(2):
            pl.semaphore_signal(
                barrier, inc=1, device_id=device((section + step) % SECTIONS, chip, other), device_id_type=MESH
            )
    pl.semaphore_signal(barrier, inc=1, device_id=device(section, chip, 1 - core), device_id_type=MESH)

    active = 0
    for index, count in enumerate(counts):
        active = jnp.where(section == index, count, active)

    def weight_copies(slot, group):
        span = pl.ds(pl.multiple_of(group * GROUP, GROUP), GROUP)
        return [
            pltpu.make_async_copy(
                wqkv_hbm.at[slot, :, pl.ds(pl.multiple_of(part * INNER + group * GROUP, GROUP), GROUP)],
                wqkv.at[slot, :, pl.ds(pl.multiple_of(part * INNER + group * GROUP, GROUP), GROUP)],
                w_sem.at[slot, group, part],
            )
            for part in range(3)
        ]

    def out_copy(slot):
        return pltpu.make_async_copy(wo_hbm.at[slot], wo.at[slot], w_sem.at[slot, 3, 0])

    @pl.loop(0, active)
    def _(slot):
        @pl.loop(0, 3)
        def _(step):
            for copy in weight_copies(slot, (first_group + step) % 3):
                copy.start()

        out_copy(slot).start()

    length = len_ref[core]
    blk_r = lax.broadcasted_iota(jnp.int32, (GROUP, GROUP), 0) // HDIM
    blk_c = lax.broadcasted_iota(jnp.int32, (GROUP, GROUP), 1) // HDIM
    bdiag[...] = jnp.where(blk_r == blk_c, 1.0 / HDIM, 0.0).astype(jnp.bfloat16)
    token = lax.broadcasted_iota(jnp.int32, (SEQ, 128), 0)
    kve[:, 128:] = jnp.where(token < length, 1.0, 0.0).astype(jnp.bfloat16)

    def low(rows):
        return lax.broadcasted_iota(jnp.int32, (rows, 128), 1) < HDIM

    def swapped(value):
        return pltpu.roll(value, HDIM, 1)

    pl.semaphore_wait(barrier, CHIPS - 1 + 2 * (SECTIONS - 1) + 1)

    @pl.when(section == 0)
    def _():
        x[0:ROWS, :] = x0_ref[0].astype(jnp.float32)
        x[ROWS:TOK, :] = x0_ref[1].astype(jnp.float32)

    @pl.when(section > 0)
    def _():
        pltpu.make_async_copy(xn, xn, h_rs).wait()
        x[...] = xn[...].astype(jnp.float32)

    def send_copy(par, h):
        target = (h + 8 * core) % CHIPS
        return target, pltpu.make_async_remote_copy(
            src_ref=snd.at[h],
            dst_ref=rcv.at[par, chip],
            send_sem=s_ss.at[h],
            recv_sem=s_rs.at[par],
            device_id=device(section, target, core),
            device_id_type=MESH,
        )

    def hop_copy(group):
        span = pl.ds(pl.multiple_of(group * 512, 512), 512)
        return pltpu.make_async_remote_copy(
            src_ref=xn.at[:, span],
            dst_ref=xn.at[:, span],
            send_sem=h_ss.at[group],
            recv_sem=h_rs,
            device_id=device((section + 1) % SECTIONS, chip, core),
            device_id_type=MESH,
        )

    def return_copy(block):
        return pltpu.make_async_remote_copy(
            src_ref=rsnd.at[block],
            dst_ref=ret.at[head],
            send_sem=r_ss.at[block],
            recv_sem=r_rs,
            device_id=device(section, block, core),
            device_id_type=MESH,
        )

    @pl.loop(0, active)
    def _(slot):
        par = slot
        xv = x[...]
        mean = jnp.mean(xv * xv, axis=-1, keepdims=True)
        gains = ng_ref[...].astype(jnp.float32)
        gain = jnp.where(slot == 0, gains[0:1], gains[1:2])
        xn[...] = (xv * lax.rsqrt(mean + EPS) * gain).astype(jnp.bfloat16)
        qks = qkg_ref[...].astype(jnp.float32)
        qk = jnp.where(slot == 0, qks[0:1], qks[1:2])
        gq = jnp.concatenate([qk[:, :HDIM] * (SCALE * LOG2E)] * 4, axis=1)
        gk = jnp.concatenate([qk[:, HDIM:]] * 4, axis=1)

        @pl.loop(0, 3)
        def _(step):
            group = (first_group + step) % 3
            for copy in weight_copies(slot, group):
                copy.wait()
            xb = xn[...]
            parts = []
            for part in range(3):
                span = pl.ds(pl.multiple_of(part * INNER + group * GROUP, GROUP), GROUP)
                parts.append(jnp.dot(xb, wqkv[slot, :, span], preferred_element_type=jnp.float32))
            q, k, v = parts
            squares = jnp.concatenate([q * q, k * k], axis=0)
            means = jnp.dot(squares.astype(jnp.bfloat16), bdiag[...], preferred_element_type=jnp.float32)
            inv = lax.rsqrt(means + EPS)
            q = q * inv[:TOK] * gq
            k = k * inv[TOK:] * gk
            for pair in range(2):
                cols = slice(128 * pair, 128 * pair + 128)
                qp, kp, vp = q[:, cols], k[:, cols], v[:, cols]
                kr, vr, qr = swapped(kp), swapped(vp), swapped(qp)
                lo = low(TOK)
                even = jnp.where(lo, kp, vr)
                odd = jnp.where(lo, kr, vp)
                lob = low(ROWS_B)
                q_even = jnp.concatenate(
                    [jnp.where(lob, qp[:ROWS_B], qr[ROWS_A:]), qp[ROWS_B:ROWS_A]], axis=0
                )
                q_odd = jnp.concatenate(
                    [jnp.where(lob, qr[:ROWS_B], qp[ROWS_A:]), qr[ROWS_B:ROWS_A]], axis=0
                )
                for parity, (kv, qq) in enumerate(((even, q_even), (odd, q_odd))):
                    h = 4 * group + 2 * pair + parity
                    snd[h, 0:TOK, :] = kv.astype(jnp.bfloat16)
                    snd[h, TOK:128, :] = qq.astype(jnp.bfloat16)
            for local in range(4):
                h = 4 * group + local
                target, copy = send_copy(par, h)

                @pl.when(target != chip)
                def _():
                    copy.start()

                @pl.when(target == chip)
                def _():
                    pltpu.make_async_copy(snd.at[h], rcv.at[par, chip], s_rs.at[par]).start()

        @pl.when(head < HEADS)
        def _():
            pltpu.make_async_copy(rcv.at[par], rcv.at[par], s_rs.at[par]).wait()
            kve[:, 0:128] = rcv[par, :, 0:TOK, :].reshape(SEQ, 128) * kve[:, 128:]

            @pl.loop(0, CHUNKS)
            def _(chunk):
                first = (row + 2 - chunk + 3 * (chunk // 2) - 2 * (chunk // 3)) % CHUNKS * BLOCKS
                qp = rcv[par, pl.ds(first, BLOCKS), TOK:128, :].astype(jnp.float32)
                qa = qp.reshape(BLOCKS * ROWS_A, 128)
                qb = swapped(qp[:, :ROWS_B, :].reshape(BLOCKS * ROWS_B, 128))
                qs = jnp.concatenate([qa, qb], axis=0)
                qs = jnp.where(low(BLOCKS * TOK), qs, 0.0).astype(jnp.bfloat16)
                scores = lax.dot_general(
                    qs, kve[:, 0:128], (((1,), (1,)), ((), ())), preferred_element_type=jnp.float32
                )
                weights = jnp.exp2(scores).astype(jnp.bfloat16)
                mixed = jnp.dot(weights, kve[...], preferred_element_type=jnp.float32)
                out = mixed[:, :128] / mixed[:, 128:]
                for local in range(BLOCKS):
                    block = first + local
                    oa = swapped(out[ROWS_A * local : ROWS_A * (local + 1)])
                    base = BLOCKS * ROWS_A + ROWS_B * local
                    ob = out[base : base + ROWS_B]
                    rsnd[block, 0:ROWS_B, :] = jnp.where(low(ROWS_B), oa[:ROWS_B], ob).astype(jnp.bfloat16)
                    rsnd[block, ROWS_B:ROWS_A, :] = oa[ROWS_B:].astype(jnp.bfloat16)
                for local in range(BLOCKS):
                    block = first + local

                    @pl.when(block != chip)
                    def _():
                        return_copy(block).start()

                    @pl.when(block == chip)
                    def _():
                        pltpu.make_async_copy(rsnd.at[block], ret.at[head], r_rs).start()

        out_copy(slot).wait()
        pltpu.make_async_copy(ret, ret, r_rs).wait()
        for pair in range(HEADS // 2):
            r0 = ret[2 * pair].astype(jnp.float32)
            r1 = ret[2 * pair + 1].astype(jnp.float32)
            cols = slice(128 * pair, 128 * pair + 128)
            att[0:ROWS_A, cols] = jnp.where(low(ROWS_A), r0, swapped(r1)).astype(jnp.bfloat16)
            att[ROWS_A:TOK, cols] = jnp.where(
                low(ROWS_B), swapped(r0)[:ROWS_B], r1[:ROWS_B]
            ).astype(jnp.bfloat16)

        @pl.loop(0, 3)
        def _(group):
            span = pl.ds(pl.multiple_of(group * 512, 512), 512)
            update = jnp.dot(att[...], wo[slot, :, span], preferred_element_type=jnp.float32)
            fresh = (x[:, span] + update).astype(jnp.bfloat16)
            x[:, span] = fresh.astype(jnp.float32)

            @pl.when((slot == active - 1) & (section < SECTIONS - 1))
            def _():
                xn[:, span] = fresh
                hop_copy(group).start()

        @pl.loop(0, HEADS)
        def _(h):
            target, copy = send_copy(par, h)

            @pl.when(target != chip)
            def _():
                copy.wait_send()

        @pl.when(head < HEADS)
        def _():
            @pl.loop(0, CHIPS)
            def _(block):
                @pl.when(block != chip)
                def _():
                    return_copy(block).wait_send()

    @pl.when(section < SECTIONS - 1)
    def _():
        @pl.loop(0, 3)
        def _(group):
            hop_copy(group).wait_send()

    @pl.when(section == SECTIONS - 1)
    def _():
        copies = []
        for owner in range(2):
            for part in range(SECTIONS):
                osnd[owner, part] = x[
                    owner * ROWS : (owner + 1) * ROWS, part * OUT_COLS : (part + 1) * OUT_COLS
                ].astype(jnp.bfloat16)
        for part in range(SECTIONS - 1):
            for owner in range(2):
                copies.append(
                    pltpu.make_async_remote_copy(
                        src_ref=osnd.at[owner, part],
                        dst_ref=orcv.at[core],
                        send_sem=o_ss.at[owner, part],
                        recv_sem=o_rs,
                        device_id=device(part, chip, owner),
                        device_id_type=MESH,
                    )
                )
        last = SECTIONS - 1
        copies.append(
            pltpu.make_async_remote_copy(
                src_ref=osnd.at[1 - core, last],
                dst_ref=orcv.at[core],
                send_sem=o_ss.at[0, last],
                recv_sem=o_rs,
                device_id=device(last, chip, 1 - core),
                device_id_type=MESH,
            )
        )
        for copy in copies:
            copy.start()
        pltpu.make_async_copy(osnd.at[core, last], orcv.at[core], o_rs).start()
        for copy in copies:
            copy.wait_send()

    pltpu.make_async_copy(orcv, orcv, o_rs).wait()
    o_ref[...] = orcv[...]


def relay_call(counts, cid, lengths, x0, norm_gain, qkv_weight, qk_gain, out_weight):
    vmem = pl.BlockSpec(memory_space=pltpu.VMEM)
    hbm = pl.BlockSpec(memory_space=pl.ANY)
    dma = pltpu.SemaphoreType.DMA
    bf16, f32 = jnp.bfloat16, jnp.float32
    return pl.pallas_call(
        functools.partial(relay, counts),
        name="relay_" + "".join(str(n) for n in counts),
        out_shape=jax.ShapeDtypeStruct((MICRO, ROWS, OUT_COLS), bf16),
        in_specs=[pl.BlockSpec(memory_space=pltpu.SMEM), vmem, vmem, hbm, vmem, hbm],
        out_specs=vmem,
        scratch_shapes=[
            pltpu.VMEM((SLOTS, D, 3 * INNER), bf16),
            pltpu.VMEM((SLOTS, INNER, D), bf16),
            pltpu.VMEM((TOK, D), f32),
            pltpu.VMEM((TOK, D), bf16),
            pltpu.VMEM((HEADS, 128, 128), bf16),
            pltpu.VMEM((2, CHIPS, 128, 128), bf16),
            pltpu.VMEM((SEQ, 256), bf16),
            pltpu.VMEM((GROUP, GROUP), bf16),
            pltpu.VMEM((CHIPS, ROWS_A, 128), bf16),
            pltpu.VMEM((HEADS, ROWS_A, 128), bf16),
            pltpu.VMEM((TOK, INNER), bf16),
            pltpu.VMEM((2, SECTIONS, ROWS, OUT_COLS), bf16),
            pltpu.VMEM((2, ROWS, OUT_COLS), bf16),
            dma((SLOTS, 4, 3)),
            dma((HEADS,)),
            dma((2,)),
            dma((CHIPS,)),
            dma,
            dma((3,)),
            dma,
            dma((2, SECTIONS)),
            dma,
        ],
        compiler_params=pltpu.CompilerParams(
            collective_id=cid, has_side_effects=True, vmem_limit_bytes=56 * 1024 * 1024
        ),
    )(lengths, x0, norm_gain, qkv_weight, qk_gain, out_weight)


PATTERNS = [p for p in itertools.product((1, 2), repeat=SECTIONS) if 1 in p and 2 in p]


def local(latents, lengths, segment_layers, norm_gain, qkv_weight, qk_gain, out_weight):
    x0, gathered = gather_call(latents, segment_layers)
    twos = gathered[:, 0, 0] > 1
    code = jnp.sum(jnp.where(twos, jnp.array([8, 4, 2, 1], jnp.int32), 0))
    index = jnp.clip(code - 1, 0, len(PATTERNS) - 1)
    branches = [functools.partial(relay_call, p, i + 1) for i, p in enumerate(PATTERNS)]
    return lax.switch(index, branches, lengths, x0, norm_gain, qkv_weight, qk_gain, out_weight)


def solution(mesh):
    return jax.shard_map(
        local,
        mesh=mesh,
        in_specs=(
            P(None, "seq", None),
            P(),
            P("section"),
            P("section", None),
            P("section", None, None),
            P("section", None),
            P("section", None, None),
        ),
        out_specs=P(None, "seq", "section"),
        check_vma=False,
    )
```
